512 devices in a mesh: dp: 128 (over y, z, core), rep: 4 (over x).
Axes of the slice: x: 4, y: 8, z: 8, core: 2. Of those that a mesh axis runs over, the one named last changes fastest.
Arguments:
- gradient_receptance: bfloat16 [128, 4, 2, 768, 768], P('dp', 'rep'), may hold values from -1000 to 1000
- gradient_factors: bfloat16 [128, 4, 2, 768, 256], P('dp', 'rep'), may hold values from -1000 to 1000
- gradient_channels: bfloat16 [128, 4, 2, 768, 16], P('dp', 'rep'), may hold values from -1000 to 1000
- primary_receptance: float32 [768, 768], P('dp'), may hold values from -0.21875 to 0.21875
- primary_factors: float32 [768, 256], P('dp'), may hold values from -0.21875 to 0.21875
- primary_channels: float32 [768, 16], P('dp'), may hold values from -1 to 1
- first_moment_receptance: float32 [768, 768], P('dp'), may hold values from -0.00390625 to 0.00390625
- first_moment_factors: float32 [768, 256], P('dp'), may hold values from -0.00390625 to 0.00390625
- first_moment_channels: float32 [768, 16], P('dp'), may hold values from -0.00390625 to 0.00390625
- second_moment_receptance: float32 [768, 768], P('dp'), may hold values from 1e-08 to 1e-06
- second_moment_factors: float32 [768, 256], P('dp'), may hold values from 1e-08 to 1e-06
- second_moment_channels: float32 [768, 16], P('dp'), may hold values from 1e-08 to 1e-06
Outputs:
- weight_receptance: bfloat16 [768, 768], replicated
- weight_lora: bfloat16 [768, 256], replicated
- weight_vectors: bfloat16 [768, 16], replicated
- new_master_receptance: float32 [768, 768], P('dp')
- new_master_lora: float32 [768, 256], P('dp')
- new_master_vectors: float32 [768, 16], P('dp')
- new_first_receptance: float32 [768, 768], P('dp')
- new_first_lora: float32 [768, 256], P('dp')
- new_first_vectors: float32 [768, 16], P('dp')
- new_second_receptance: float32 [768, 768], P('dp')
- new_second_lora: float32 [768, 256], P('dp')
- new_second_vectors: float32 [768, 16], P('dp')
The draws below stay inside these ranges and needn't reach their ends.
All inputs are finite; a program needn't handle non-finite values.
Results may differ from the reference program's by a relative error of at most 0.001.
Values may be sent and summed in bfloat16 or wider, within the bound.
A program may use at most 64 MiB of HBM per device.

```python
import math
import jax
import jax.numpy as jnp
from jax import lax

MODEL_WIDTH = 768
FACTOR_RANK = 64
NV = 16
MB = 2
STEP = 20
N_DP = 128
N_REP = 4


def gradient_draw(key, columns, group_tag):
    row_key = jax.random.fold_in(key, 7001)
    pair_key = jax.random.fold_in(key, 7002)
    column_key = jax.random.fold_in(key, 7004 + 10 * group_tag)
    noise_key = jax.random.fold_in(key, 7005 + 10 * group_tag)
    shared_key = jax.random.fold_in(key, 7006 + 10 * group_tag)
    full_shape = (N_DP, N_REP, MB, MODEL_WIDTH, columns)
    row_scale = jnp.exp(jax.random.uniform(row_key, (MODEL_WIDTH,), jnp.float32, -2.3, 2.3))
    column_scale = jnp.exp(jax.random.uniform(column_key, (columns,), jnp.float32, 0.0, 2.3))
    random_part = jnp.clip(jax.random.normal(noise_key, full_shape, jnp.float32), -6.0, 6.0)
    shared = 0.5 * jnp.clip(jax.random.normal(shared_key, (MODEL_WIDTH, columns), jnp.float32), -6.0, 6.0)
    owner_block = jax.random.permutation(pair_key, N_DP)
    row_block = jnp.arange(MODEL_WIDTH) // (MODEL_WIDTH // N_DP)
    loudness = jnp.where(owner_block[:, None] == row_block[None, :], 5.5, 1.0).astype(jnp.float32)
    values = random_part * loudness[:, None, None, :, None] * row_scale[:, None] * column_scale[None, :] + shared
    return jnp.clip(values, -1000.0, 1000.0)


def draw_gradient_receptance(key, part):
    return gradient_draw(key, MODEL_WIDTH, 1).astype(jnp.bfloat16)


def draw_gradient_factors(key, part):
    return gradient_draw(key, 4 * FACTOR_RANK, 2).astype(jnp.bfloat16)


def draw_gradient_channels(key, part):
    return gradient_draw(key, NV, 3).astype(jnp.bfloat16)


def level_of(stream_key, dims, split, smallest, high):
    factor_of, own = 1.0, jax.random.fold_in(stream_key, 6)
    for dim, parts in split:
        heights = jnp.exp(jax.random.uniform(jax.random.fold_in(own, dim), (parts,), jnp.float32, smallest / len(split), high / len(split)))
        factor_of = factor_of * jnp.repeat(heights, dims[dim] // parts).reshape([-1 if axis == dim else 1 for axis in range(len(dims))])
    return factor_of


def scatter_about(rng, shape, deviation, reach, split=(), kind=jnp.bfloat16):
    level = level_of(rng, shape, split, -0.22, 0.18) if split else 1.0
    result = jax.random.normal(rng, shape, jnp.float32) * deviation * level
    return jnp.minimum(jnp.maximum(result, -reach), reach).astype(kind)


def setup_inputs(seed: int = 0) -> dict:
    keys = jax.random.split(jax.random.key(seed), 13)
    return {
        "gradient_receptance": draw_gradient_receptance(jax.random.fold_in(keys[12], 71), 0),
        "gradient_factors": draw_gradient_factors(jax.random.fold_in(keys[12], 71), 0),
        "gradient_channels": draw_gradient_channels(jax.random.fold_in(keys[12], 71), 0),
        "primary_receptance": scatter_about(keys[3], (MODEL_WIDTH, MODEL_WIDTH), MODEL_WIDTH ** -0.5, 0.21875, ((0, 128),), jnp.float32),
        "primary_factors": scatter_about(keys[4], (MODEL_WIDTH, 4 * FACTOR_RANK), MODEL_WIDTH ** -0.5, 0.21875, ((0, 128),), jnp.float32),
        "primary_channels": jnp.clip(jax.random.uniform(keys[5], (MODEL_WIDTH, NV), jnp.float32, -1.0, 1.0) * level_of(keys[5], (MODEL_WIDTH, NV), ((0, 128),), -0.4, 0.0), -1.0, 1.0),
        "first_moment_receptance": scatter_about(keys[6], (MODEL_WIDTH, MODEL_WIDTH), 0.0003, 0.00390625, ((0, 128),), jnp.float32),
        "first_moment_factors": scatter_about(keys[7], (MODEL_WIDTH, 4 * FACTOR_RANK), 0.0003, 0.00390625, ((0, 128),), jnp.float32),
        "first_moment_channels": scatter_about(keys[8], (MODEL_WIDTH, NV), 0.0003, 0.00390625, ((0, 128),), jnp.float32),
        "second_moment_receptance": jnp.clip(jnp.exp(math.log(9.999999974752427e-07) - 4.6051702 * jax.random.uniform(keys[9], (MODEL_WIDTH, MODEL_WIDTH), jnp.float32) ** level_of(keys[9], (MODEL_WIDTH, MODEL_WIDTH), ((0, 128),), -0.2, 0.2)), 9.99999993922529e-09, 9.999999974752427e-07),
        "second_moment_factors": jnp.clip(jnp.exp(math.log(9.999999974752427e-07) - 4.6051702 * jax.random.uniform(keys[10], (MODEL_WIDTH, 4 * FACTOR_RANK), jnp.float32) ** level_of(keys[10], (MODEL_WIDTH, 4 * FACTOR_RANK), ((0, 128),), -0.2, 0.2)), 9.99999993922529e-09, 9.999999974752427e-07),
        "second_moment_channels": jnp.clip(jnp.exp(math.log(9.999999974752427e-07) - 4.6051702 * jax.random.uniform(keys[11], (MODEL_WIDTH, NV), jnp.float32) ** level_of(keys[11], (MODEL_WIDTH, NV), ((0, 128),), -0.2, 0.2)), 9.99999993922529e-09, 9.999999974752427e-07),
    }


beta_one = 0.9
beta_two = 0.99
adam_eps = 1e-08
learn_rate = 0.001
weight_decay_rate = 0.1
max_norm = 1.0
norm_eps = 1e-06

def combine_device_group(gradient):

    def accumulate(total, block):
        return (total + lax.optimization_barrier(jnp.sum(block, axis=(0, 1), dtype=jnp.float32)), None)
    start = jnp.zeros(gradient.shape[3:], jnp.float32)
    total, unused = lax.scan(accumulate, start, gradient)
    return total

def decoupled_adam_step(gradient, master, first, second, decay):
    new_first = beta_one * first + (1.0 - beta_one) * gradient
    new_second = beta_two * second + (1.0 - beta_two) * gradient * gradient
    update = new_first / (1.0 - beta_one ** STEP) / (jnp.sqrt(new_second / (1.0 - beta_two ** STEP)) + adam_eps)
    new_master = master - learn_rate * (update + decay * master)
    return (new_master, new_first, new_second)

def reference(gradient_receptance, gradient_factors, gradient_channels, primary_receptance, primary_factors, primary_channels, first_moment_receptance, first_moment_factors, first_moment_channels, second_moment_receptance, second_moment_factors, second_moment_channels):
    partial_sums = [combine_device_group(gradient_receptance), combine_device_group(gradient_factors), combine_device_group(gradient_channels)]
    square_sum = jnp.sum(partial_sums[0] * partial_sums[0]) + jnp.sum(partial_sums[1] * partial_sums[1]) + jnp.sum(partial_sums[2] * partial_sums[2])
    clipping_ratio = jnp.minimum(1.0, max_norm / (jnp.sqrt(square_sum) + norm_eps))
    receptance_part = decoupled_adam_step(clipping_ratio * partial_sums[0], primary_receptance, first_moment_receptance, second_moment_receptance, weight_decay_rate)
    lowrank_factors = decoupled_adam_step(clipping_ratio * partial_sums[1], primary_factors, first_moment_factors, second_moment_factors, weight_decay_rate)
    channel_vectors = decoupled_adam_step(clipping_ratio * partial_sums[2], primary_channels, first_moment_channels, second_moment_channels, 0.0)
    return (receptance_part[0].astype(jnp.bfloat16), lowrank_factors[0].astype(jnp.bfloat16), channel_vectors[0].astype(jnp.bfloat16), receptance_part[0], lowrank_factors[0], channel_vectors[0], receptance_part[1], lowrank_factors[1], channel_vectors[1], receptance_part[2], lowrank_factors[2], channel_vectors[2])
```

```python
import functools

import jax
import jax.numpy as jnp
from jax import lax
from jax.experimental import pallas as pl
from jax.experimental.pallas import tpu as pltpu
from jax.sharding import PartitionSpec as P

STEP = 20
NZ = 8

beta_one = 0.9
beta_two = 0.99
adam_eps = 1e-08
learn_rate = 0.001
weight_decay_rate = 0.1
max_norm = 1.0
norm_eps = 1e-06

MESH = pl.DeviceIdType.MESH
f32 = jnp.float32
bf16 = jnp.bfloat16

STREAMS = ((1, 0), (1, 1), (-1, 1), (-1, 0))
LONG = (True, False, True, False)


def adam(g, master, first, second, decay):
    new_first = beta_one * first + (1.0 - beta_one) * g
    new_second = beta_two * second + (1.0 - beta_two) * g * g
    update = (
        new_first
        / (1.0 - beta_one**STEP)
        / (jnp.sqrt(new_second / (1.0 - beta_two**STEP)) + adam_eps)
    )
    new_master = master - learn_rate * (update + decay * master)
    return new_master, new_first, new_second


def kernel(
    ny, nz, nx,
    rec, fac, chg, mrec, mfac, frec, ffac, srec, sfac, chs,
    wrec, wfac, wch, omrec, omfac, ofrec, offac, osrec, osfac, och,
    own, part, chp, acc, rbuf, zs, zr, xb, sb, sws, swr, n1, n2, hb, ar, bb, zag, asm, w,
    own_sem, pair_s, pair_r, chp_s, chp_r, rs_s, rs_r, z_s, z_r, x_s, x_r, sw_sem,
    n1_s, n1_r, n2_s, n2_r, ag_sem, zag_s, zag_r, yag_s, yag_r, pc_s, pc_r, po_s, po_r,
):
    cr = 12 * nz
    half = ny // 2
    dp = lax.axis_index("dp")
    x = lax.axis_index("rep")
    c = lax.rem(dp, 2)
    z = lax.rem(dp // 2, nz)
    y = dp // (2 * nz)
    d = 1 - c

    def at(yy, zz, cc, xx):
        return ((yy * nz + zz) * 2 + cc, xx)

    def yo(o):
        return lax.rem(y + o + ny, ny)

    def zo(o):
        return lax.rem(z + o, nz)

    def xo(o):
        return lax.rem(x + o, nx)

    def remote(src, dst, ss, rs, dev):
        return pltpu.make_async_remote_copy(
            src_ref=src, dst_ref=dst, send_sem=ss, recv_sem=rs, device_id=dev, device_id_type=MESH
        )

    partner = at(y, z, d, x)

    own0 = pltpu.make_async_copy(
        rec.at[0, 0, :, :, pl.ds(pl.multiple_of(c * 512, 256), 256)], own.at[0], own_sem.at[0]
    )
    own0.start()

    @pl.when(c == 0)
    def _():
        pltpu.make_async_copy(rec.at[0, 0, :, :, pl.ds(256, 256)], own.at[1], own_sem.at[1]).start()

    @pl.when(c == 1)
    def _():
        pltpu.make_async_copy(fac.at[0, 0], own.at[1], own_sem.at[1]).start()

    barrier = pltpu.get_barrier_semaphore()
    peers = [partner]
    for o in range(1, nz):
        peers += [at(y, zo(o), c, x), at(y, zo(o), d, x)]
    for o in range(1, ny):
        peers.append(at(yo(o), z, c, x))
    for o in range(1, nx):
        peers.append(at(y, z, c, xo(o)))
    for dev in peers:
        pl.semaphore_signal(barrier, inc=1, device_id=dev, device_id_type=MESH)
    pl.semaphore_wait(barrier, len(peers))

    order = [half]
    for o in range(half - 1, 0, -1):
        order += [o, ny - o]
    order.append(0)

    def rows_of(k):
        return pl.ds(pl.multiple_of(k * cr, 16), cr)

    def pair0(i):
        k = yo(order[i])
        return remote(
            rec.at[0, 0, :, rows_of(k), pl.ds(pl.multiple_of(d * 512, 256), 256)],
            part.at[0, :, rows_of(k), :], pair_s.at[0, i], pair_r.at[0, i], partner,
        )

    def pair1(i, to_fac):
        k = yo(order[i])
        if to_fac:
            src = fac.at[0, 0, :, rows_of(k), :]
        else:
            src = rec.at[0, 0, :, rows_of(k), pl.ds(256, 256)]
        return remote(src, part.at[1, :, rows_of(k), :], pair_s.at[1, i], pair_r.at[1, i], partner)

    chc = remote(chg, chp, chp_s, chp_r, partner)
    for i in range(ny):
        pair0(i).start()

        @pl.when(d == 1)
        def _():
            pair1(i, True).start()

        @pl.when(d == 0)
        def _():
            pair1(i, False).start()

        if i == 0:
            chc.start()

    own0.wait()
    pltpu.make_async_copy(fac.at[0, 0], own.at[1], own_sem.at[1]).wait()
    chc.wait_recv()

    def chip_sum(i):
        k = yo(order[i])
        pair0(i).wait_recv()
        pair1(i, True).wait_recv()
        for h in range(2):
            r = rows_of(k)
            s = (own[h, 0, r, :].astype(f32) + own[h, 1, r, :].astype(f32)) + (
                part[h, 0, r, :].astype(f32) + part[h, 1, r, :].astype(f32)
            )
            acc[k, h, 0:cr, :] = s
        r8 = pl.ds(pl.multiple_of(k * nz, nz), nz)
        acc[k, 0, cr : cr + nz, :] = chg[r8, :] + chp[r8, :]

    def nrow(h):
        return cr + nz if h == 0 else cr

    def rs(st, s):
        dirn, h = STREAMS[st]
        r = pl.ds(0, nrow(h))
        return remote(
            acc.at[yo(dirn * (half - s)), h, r, :], rbuf.at[st, s, r, :],
            rs_s.at[st, s], rs_r.at[st, s], at(yo(dirn), z, c, x),
        )

    chip_sum(0)
    rs(0, 0).start()
    rs(2, 0).start()
    done = 1
    for s in range(1, half):
        chip_sum(done)
        if s == 1:
            rs(1, 1).start()
        chip_sum(done + 1)
        if s == 1:
            rs(3, 1).start()
        done += 2
        for st in (0, 2, 1, 3):
            if s == 1 and not LONG[st]:
                continue
            dirn, h = STREAMS[st]
            rs(st, s - 1).wait_recv()
            k = yo(dirn * (half - s))
            acc[k, h, 0 : nrow(h), :] += rbuf[st, s - 1, 0 : nrow(h), :]
            rs(st, s).start()
    chip_sum(done)
    zs[:, 8:16, :] = jnp.zeros((nz, 8, 512), f32)
    for h, sts in ((0, (0, 3)), (1, (2, 1))):
        for st in sts:
            rs(st, half - 1).wait_recv()
        n = nrow(h)
        acc[y, h, 0:n, :] = acc[y, h, 0:n, :] + (
            rbuf[sts[0], half - 1, 0:n, :] + rbuf[sts[1], half - 1, 0:n, :]
        )
        for zz in range(nz):
            zs[zz, 0:12, h * 256 : (h + 1) * 256] = acc[y, h, 12 * zz : 12 * zz + 12, :]
            if h == 0:
                zs[zz, 12:13, 0:256] = acc[y, 0, cr + zz : cr + zz + 1, :]

    far = sorted(range(1, nz), key=lambda o: -min(o, nz - o))

    def zc(o):
        return remote(zs.at[zo(o)], zr.at[o - 1], z_s.at[o - 1], z_r.at[o - 1], at(y, zo(o), c, x))

    for o in far:
        zc(o).start()
    total = zs[z]
    for o in reversed(far):
        zc(o).wait_recv()
        total = total + zr[o - 1]
    xb[x] = total

    def xc(o):
        return remote(xb.at[x], xb.at[x], x_s.at[o - 1], x_r.at[o - 1], at(y, z, c, xo(o)))

    for o in range(1, nx):
        xc(o).start()
    for o in range(1, nx):
        xc(o).wait_recv()
    total = xb[0]
    for o in range(1, nx):
        total = total + xb[o]
    sb[...] = total

    low = sb[0:6, :]
    high = sb[6:12, :]
    mine = jnp.where(c == 0, low, high)
    sws[0:6, :] = jnp.where(c == 0, high, low)
    sws[6:8, :] = jnp.zeros((2, 512), f32)
    swap = remote(sws, swr, sw_sem.at[0], sw_sem.at[1], partner)
    swap.start()

    my_ch = jnp.where(c == 0, sb[12:13, 0:128], sb[12:13, 128:256])
    sq = sb[0:8, :] * sb[0:8, :]
    sq = sq[:, 0:128] + sq[:, 128:256] + (sq[:, 256:384] + sq[:, 384:512])
    sh = sb[8:16, :] * sb[8:16, :]
    sh = sh[:, 0:128] + sh[:, 128:256] + (sh[:, 256:384] + sh[:, 384:512])
    row = lax.broadcasted_iota(jnp.int32, (8, 128), 0)
    sh = jnp.where(row < 4, sh, 0.0)
    ch_sq = jnp.where(row == 0, jnp.broadcast_to(my_ch * my_ch, (8, 128)), 0.0)
    n1[0] = sq + sh + ch_sq

    def n1c(o, e):
        i = 2 * o + e
        dev = at(y, zo(o), c if e == 0 else d, x)
        return remote(n1.at[0], n1.at[i], n1_s.at[i], n1_r.at[i], dev)

    n1_list = [(o, e) for o in [*far, 0] for e in range(2) if (o, e) != (0, 0)]
    for o, e in n1_list:
        n1c(o, e).start()
    for o, e in n1_list:
        n1c(o, e).wait_recv()
    part_sum = n1[0]
    for i in range(1, 2 * nz):
        part_sum = part_sum + n1[i]
    n2[0] = part_sum

    def n2c(o):
        return remote(n2.at[0], n2.at[o], n2_s.at[o], n2_r.at[o], at(yo(o), z, c, x))

    for o in range(1, ny):
        n2c(o).start()
    swap.wait_recv()
    for o in range(1, ny):
        n2c(o).wait_recv()
    part_sum = n2[0]
    for o in range(1, ny):
        part_sum = part_sum + n2[o]
    square_sum = jnp.sum(jnp.sum(part_sum, axis=1, keepdims=True), axis=0, keepdims=True)
    clip = jnp.minimum(1.0, max_norm / (jnp.sqrt(square_sum) + norm_eps))

    theirs = swr[0:6, :]
    gl = clip * jnp.where(c == 0, mine, theirs)
    gr = clip * jnp.where(c == 0, theirs, mine)
    nm, nf, ns = adam(gl, mrec[:, 0:512], frec[:, 0:512], srec[:, 0:512], weight_decay_rate)
    omrec[:, 0:512] = nm
    ofrec[:, 0:512] = nf
    osrec[:, 0:512] = ns
    hb[0, 0:6, :] = nm
    nm, nf, ns = adam(
        gr[:, 0:256], mrec[:, 512:768], frec[:, 512:768], srec[:, 512:768], weight_decay_rate
    )
    omrec[:, 512:768] = nm
    ofrec[:, 512:768] = nf
    osrec[:, 512:768] = ns
    hb[1, 0:6, 0:256] = nm
    nm, nf, ns = adam(gr[:, 256:512], mfac[...], ffac[...], sfac[...], weight_decay_rate)
    omfac[...] = nm
    offac[...] = nf
    osfac[...] = ns
    hb[1, 0:6, 256:512] = nm
    nm, nf, ns = adam(clip * my_ch, chs[0:1, :], chs[1:2, :], chs[2:3, :], 0.0)
    och[0:1, :] = nm
    och[1:2, :] = nf
    och[2:3, :] = ns
    for h in range(2):
        hb[h, 6:8, :] = jnp.zeros((2, 512), f32)
        hb[h, 6:7, 0:128] = nm

    aswap = remote(hb.at[d], ar, ag_sem.at[0], ag_sem.at[1], partner)
    aswap.start()
    bb[8:16, :] = jnp.zeros((8, 512), f32)
    asm[cr : cr + 16, :] = jnp.zeros((16, 512), f32)
    aswap.wait_recv()
    kept = hb[c]
    got = ar[...]
    r0 = jnp.where(c == 0, kept, got)
    r1 = jnp.where(c == 0, got, kept)
    bb[0:6, :] = r0[0:6, :]
    bb[6:12, :] = r1[0:6, :]
    bb[12:13, 0:128] = r0[6:7, 0:128]
    bb[12:13, 128:256] = r1[6:7, 0:128]
    zag[z] = bb[...].astype(bf16)

    def zg(o):
        return remote(zag.at[z], zag.at[z], zag_s.at[o - 1], zag_r.at[o - 1], at(y, zo(o), c, x))

    for o in far:
        zg(o).start()
    for o in reversed(far):
        zg(o).wait_recv()
    for zz in range(nz):
        blk = zag[zz].astype(f32)
        asm[12 * zz : 12 * zz + 12, :] = blk[0:12, :]
        asm[cr + zz : cr + zz + 1, 0:256] = blk[12:13, 0:256]
    w[c, y, 0] = asm[:, 0:256].astype(bf16)
    w[c, y, 1] = asm[:, 256:512].astype(bf16)

    def grow(h):
        return cr + 16 if h == 0 else cr

    def yg(st, s):
        dirn, h = STREAMS[st]
        blk = w.at[c, yo(-dirn * s), h, pl.ds(0, grow(h)), :]
        return remote(blk, blk, yag_s.at[st, s], yag_r.at[st, s], at(yo(dirn), z, c, x))

    def to_partner(k, h, ss, rr):
        blk = w.at[c, k, h, pl.ds(0, cr), :]
        return remote(blk, blk, ss, rr, partner)

    def pc(st, s):
        dirn, h = STREAMS[st]
        return to_partner(yo(-dirn * (s + 1)), h, pc_s.at[st, s], pc_r.at[st, s])

    def po(h):
        return to_partner(y, h, po_s.at[h], po_r.at[h])

    steps = [half if v else half - 1 for v in LONG]
    for st in (0, 2, 1, 3):
        yg(st, 0).start()
    po(0).start()
    po(1).start()
    for s in range(half):
        for st in (0, 2, 1, 3):
            if s < steps[st]:
                yg(st, s).wait_recv()
                if s + 1 < steps[st]:
                    yg(st, s + 1).start()
                pc(st, s).start()
    for h in range(2):
        po(h).wait_recv()
    for st in range(4):
        for s in range(steps[st]):
            pc(st, s).wait_recv()
    for k in range(ny):
        r = slice(cr * k, cr * k + cr)
        wrec[r, 0:256] = w[0, k, 0, 0:cr, :]
        wrec[r, 256:512] = w[0, k, 1, 0:cr, :]
        wrec[r, 512:768] = w[1, k, 0, 0:cr, :]
        wfac[r, :] = w[1, k, 1, 0:cr, :]
        wch[nz * k : nz * k + nz, :] = w[c, k, 0, cr : cr + 16, :].astype(f32)[0:nz, :]

    for i in range(ny):
        pair0(i).wait_send()
        pair1(i, True).wait_send()
    chc.wait_send()
    for st in range(4):
        for s in range(0 if LONG[st] else 1, half):
            rs(st, s).wait_send()
        for s in range(steps[st]):
            yg(st, s).wait_send()
            pc(st, s).wait_send()
    for o in range(1, nz):
        zc(o).wait_send()
        zg(o).wait_send()
    for o in range(1, nx):
        xc(o).wait_send()
    for o, e in n1_list:
        n1c(o, e).wait_send()
    for o in range(1, ny):
        n2c(o).wait_send()
    swap.wait_send()
    aswap.wait_send()
    for h in range(2):
        po(h).wait_send()


def body(ny, nz, nx, rec, fac, chan, mrec, mfac, mch, frec, ffac, fch, srec, sfac, sch):
    cr = 12 * nz
    rows = cr * ny
    sd = jax.ShapeDtypeStruct
    chg = jnp.sum(chan, axis=(0, 1, 2), dtype=f32).reshape(ny * nz, 2, 96)
    chg = jnp.pad(chg, ((0, 0), (0, 0), (0, 32))).reshape(ny * nz, 256)
    chs = jnp.pad(jnp.stack([mch, fch, sch]).reshape(3, 96), ((0, 0), (0, 32)))
    vm = pl.BlockSpec(memory_space=pltpu.VMEM)
    hbm = pl.BlockSpec(memory_space=pl.ANY)
    dma = pltpu.SemaphoreType.DMA
    half = ny // 2
    V = pltpu.VMEM
    out = pl.pallas_call(
        functools.partial(kernel, ny, nz, nx),
        out_shape=(
            sd((rows, 768), bf16), sd((rows, 256), bf16), sd((ny * nz, 256), f32),
            sd((6, 768), f32), sd((6, 256), f32), sd((6, 768), f32), sd((6, 256), f32),
            sd((6, 768), f32), sd((6, 256), f32), sd((3, 128), f32),
        ),
        in_specs=[hbm, hbm] + [vm] * 8,
        out_specs=(vm,) * 10,
        scratch_shapes=[
            V((2, 2, rows, 256), bf16), V((2, 2, rows, 256), bf16), V((ny * nz, 256), f32),
            V((ny, 2, cr + nz, 256), f32), V((4, half, cr + nz, 256), f32),
            V((nz, 16, 512), f32), V((nz - 1, 16, 512), f32), V((nx, 16, 512), f32),
            V((16, 512), f32), V((8, 512), f32), V((8, 512), f32),
            V((2 * nz, 8, 128), f32), V((ny, 8, 128), f32), V((2, 8, 512), f32), V((8, 512), f32),
            V((16, 512), f32), V((nz, 16, 512), bf16), V((cr + 16, 512), f32),
            V((2, ny, 2, cr + 16, 256), bf16),
            dma((2,)), dma((2, ny)), dma((2, ny)), dma, dma,
            dma((4, half)), dma((4, half)), dma((nz - 1,)), dma((nz - 1,)),
            dma((nx - 1,)), dma((nx - 1,)), dma((2,)),
            dma((2 * nz,)), dma((2 * nz,)), dma((ny,)), dma((ny,)), dma((2,)),
            dma((nz - 1,)), dma((nz - 1,)), dma((4, half)), dma((4, half)),
            dma((4, half)), dma((4, half)), dma((2,)), dma((2,)),
        ],
        compiler_params=pltpu.CompilerParams(
            collective_id=0, has_side_effects=True, vmem_limit_bytes=48 << 20
        ),
    )(rec, fac, chg, mrec, mfac, frec, ffac, srec, sfac, chs)
    wrec, wfac, wch, omrec, omfac, ofrec, offac, osrec, osfac, och = out
    wch = wch.reshape(ny * nz, 2, 128)[:, :, :96].reshape(rows, 16).astype(bf16)
    och = och[:, :96].reshape(3, 6, 16)
    return (
        wrec, wfac, wch,
        omrec, omfac, och[0],
        ofrec, offac, och[1],
        osrec, osfac, och[2],
    )


def solution(mesh, nz=NZ):
    nx = mesh.shape["rep"]
    ny = mesh.shape["dp"] // (2 * nz)
    grad = P("dp", "rep", None, None, None)
    row = P("dp", None)
    return jax.shard_map(
        functools.partial(body, ny, nz, nx),
        mesh=mesh,
        in_specs=(grad,) * 3 + (row,) * 9,
        out_specs=(P(),) * 3 + (row,) * 9,
        check_vma=False,
    )
```

```python
import functools

import jax
import jax.numpy as jnp
from jax import lax
from jax.experimental import pallas as pl
from jax.experimental.pallas import tpu as pltpu
from jax.sharding import PartitionSpec as P

STEP = 20
NZ = 8

beta_one = 0.9
beta_two = 0.99
adam_eps = 1e-08
learn_rate = 0.001
weight_decay_rate = 0.1
max_norm = 1.0
norm_eps = 1e-06

MESH = pl.DeviceIdType.MESH
f32 = jnp.float32
bf16 = jnp.bfloat16

STREAMS = ((1, 0), (1, 1), (-1, 1), (-1, 0))
LONG = (True, False, True, False)


def adam(g, master, first, second, decay):
    new_first = beta_one * first + (1.0 - beta_one) * g
    new_second = beta_two * second + (1.0 - beta_two) * g * g
    update = (
        new_first
        / (1.0 - beta_one**STEP)
        / (jnp.sqrt(new_second / (1.0 - beta_two**STEP)) + adam_eps)
    )
    new_master = master - learn_rate * (update + decay * master)
    return new_master, new_first, new_second


def kernel(
    ny, nz, nx,
    rec, fac, chg, mrec, mfac, mch, frec, ffac, fch, srec, sfac, sch,
    wrec, wfac, wch, omrec, omfac, omch, ofrec, offac, ofch, osrec, osfac, osch,
    chs, och, own, part, chp, acc, rbuf, zs, zr, xb, sb, sws, swr, n1, n2, hb, ar, bb, zag, asm, w,
    own_sem, pair_s, pair_r, chp_s, chp_r, rs_s, rs_r, z_s, z_r, x_s, x_r, sw_sem,
    n1_s, n1_r, n2_s, n2_r, ag_sem, zag_s, zag_r, yag_s, yag_r, pc_s, pc_r, po_s, po_r,
):
    cr = 12 * nz
    half = ny // 2
    dp = lax.axis_index("dp")
    x = lax.axis_index("rep")
    c = lax.rem(dp, 2)
    z = lax.rem(dp // 2, nz)
    y = dp // (2 * nz)
    d = 1 - c

    def at(yy, zz, cc, xx):
        return ((yy * nz + zz) * 2 + cc, xx)

    def yo(o):
        return lax.rem(y + o + ny, ny)

    def zo(o):
        return lax.rem(z + o, nz)

    def xo(o):
        return lax.rem(x + o, nx)

    def remote(src, dst, ss, rs, dev):
        return pltpu.make_async_remote_copy(
            src_ref=src, dst_ref=dst, send_sem=ss, recv_sem=rs, device_id=dev, device_id_type=MESH
        )

    partner = at(y, z, d, x)

    own0 = pltpu.make_async_copy(
        rec.at[0, 0, :, :, pl.ds(pl.multiple_of(c * 512, 256), 256)], own.at[0], own_sem.at[0]
    )
    own0.start()

    @pl.when(c == 0)
    def _():
        pltpu.make_async_copy(rec.at[0, 0, :, :, pl.ds(256, 256)], own.at[1], own_sem.at[1]).start()

    @pl.when(c == 1)
    def _():
        pltpu.make_async_copy(fac.at[0, 0], own.at[1], own_sem.at[1]).start()

    barrier = pltpu.get_barrier_semaphore()
    peers = [partner]
    for o in range(1, nz):
        peers += [at(y, zo(o), c, x), at(y, zo(o), d, x)]
    for o in range(1, ny):
        peers.append(at(yo(o), z, c, x))
    for o in range(1, nx):
        peers.append(at(y, z, c, xo(o)))
    for dev in peers:
        pl.semaphore_signal(barrier, inc=1, device_id=dev, device_id_type=MESH)
    chs[...] = jnp.zeros_like(chs)
    for i, ref in enumerate((mch, fch, sch)):
        for r in range(6):
            chs[i : i + 1, 16 * r : 16 * r + 16] = ref[r : r + 1, :]
    pl.semaphore_wait(barrier, len(peers))

    order = [half]
    for o in range(half - 1, 0, -1):
        order += [o, ny - o]
    order.append(0)

    def rows_of(k):
        return pl.ds(pl.multiple_of(k * cr, 16), cr)

    def pair0(i):
        k = yo(order[i])
        return remote(
            rec.at[0, 0, :, rows_of(k), pl.ds(pl.multiple_of(d * 512, 256), 256)],
            part.at[0, :, rows_of(k), :], pair_s.at[0, i], pair_r.at[0, i], partner,
        )

    def pair1(i, to_fac):
        k = yo(order[i])
        if to_fac:
            src = fac.at[0, 0, :, rows_of(k), :]
        else:
            src = rec.at[0, 0, :, rows_of(k), pl.ds(256, 256)]
        return remote(src, part.at[1, :, rows_of(k), :], pair_s.at[1, i], pair_r.at[1, i], partner)

    chc = remote(chg, chp, chp_s, chp_r, partner)
    for i in range(ny):
        pair0(i).start()

        @pl.when(d == 1)
        def _():
            pair1(i, True).start()

        @pl.when(d == 0)
        def _():
            pair1(i, False).start()

        if i == 0:
            chc.start()

    own0.wait()
    pltpu.make_async_copy(fac.at[0, 0], own.at[1], own_sem.at[1]).wait()
    chc.wait_recv()

    def chip_sum(i):
        k = yo(order[i])
        pair0(i).wait_recv()
        pair1(i, True).wait_recv()
        for h in range(2):
            r = rows_of(k)
            s = (own[h, 0, r, :].astype(f32) + own[h, 1, r, :].astype(f32)) + (
                part[h, 0, r, :].astype(f32) + part[h, 1, r, :].astype(f32)
            )
            acc[k, h, 0:cr, :] = s
        r8 = pl.ds(pl.multiple_of(k * nz, nz), nz)
        acc[k, 0, cr : cr + nz, :] = chg[r8, :] + chp[r8, :]

    def nrow(h):
        return cr + nz if h == 0 else cr

    def rs(st, s):
        dirn, h = STREAMS[st]
        r = pl.ds(0, nrow(h))
        return remote(
            acc.at[yo(dirn * (half - s)), h, r, :], rbuf.at[st, s, r, :],
            rs_s.at[st, s], rs_r.at[st, s], at(yo(dirn), z, c, x),
        )

    chip_sum(0)
    rs(0, 0).start()
    rs(2, 0).start()
    done = 1
    for s in range(1, half):
        chip_sum(done)
        if s == 1:
            rs(1, 1).start()
        chip_sum(done + 1)
        if s == 1:
            rs(3, 1).start()
        done += 2
        for st in (0, 2, 1, 3):
            if s == 1 and not LONG[st]:
                continue
            dirn, h = STREAMS[st]
            rs(st, s - 1).wait_recv()
            k = yo(dirn * (half - s))
            acc[k, h, 0 : nrow(h), :] += rbuf[st, s - 1, 0 : nrow(h), :]
            rs(st, s).start()
    chip_sum(done)
    zs[:, 8:16, :] = jnp.zeros((nz, 8, 512), f32)
    for h, sts in ((0, (0, 3)), (1, (2, 1))):
        for st in sts:
            rs(st, half - 1).wait_recv()
        n = nrow(h)
        acc[y, h, 0:n, :] = acc[y, h, 0:n, :] + (
            rbuf[sts[0], half - 1, 0:n, :] + rbuf[sts[1], half - 1, 0:n, :]
        )
        for zz in range(nz):
            zs[zz, 0:12, h * 256 : (h + 1) * 256] = acc[y, h, 12 * zz : 12 * zz + 12, :]
            if h == 0:
                zs[zz, 12:13, 0:256] = acc[y, 0, cr + zz : cr + zz + 1, :]

    far = sorted(range(1, nz), key=lambda o: -min(o, nz - o))

    def zc(o):
        return remote(zs.at[zo(o)], zr.at[o - 1], z_s.at[o - 1], z_r.at[o - 1], at(y, zo(o), c, x))

    for o in far:
        zc(o).start()
    total = zs[z]
    for o in reversed(far):
        zc(o).wait_recv()
        total = total + zr[o - 1]
    xb[x] = total

    def xc(o):
        return remote(xb.at[x], xb.at[x], x_s.at[o - 1], x_r.at[o - 1], at(y, z, c, xo(o)))

    for o in range(1, nx):
        xc(o).start()
    for o in range(1, nx):
        xc(o).wait_recv()
    total = xb[0]
    for o in range(1, nx):
        total = total + xb[o]
    sb[...] = total

    low = sb[0:6, :]
    high = sb[6:12, :]
    mine = jnp.where(c == 0, low, high)
    sws[0:6, :] = jnp.where(c == 0, high, low)
    sws[6:8, :] = jnp.zeros((2, 512), f32)
    swap = remote(sws, swr, sw_sem.at[0], sw_sem.at[1], partner)
    swap.start()

    my_ch = jnp.where(c == 0, sb[12:13, 0:128], sb[12:13, 128:256])
    sq = sb[0:8, :] * sb[0:8, :]
    sq = sq[:, 0:128] + sq[:, 128:256] + (sq[:, 256:384] + sq[:, 384:512])
    sh = sb[8:16, :] * sb[8:16, :]
    sh = sh[:, 0:128] + sh[:, 128:256] + (sh[:, 256:384] + sh[:, 384:512])
    row = lax.broadcasted_iota(jnp.int32, (8, 128), 0)
    sh = jnp.where(row < 4, sh, 0.0)
    ch_sq = jnp.where(row == 0, jnp.broadcast_to(my_ch * my_ch, (8, 128)), 0.0)
    n1[0] = sq + sh + ch_sq

    def n1c(o, e):
        i = 2 * o + e
        dev = at(y, zo(o), c if e == 0 else d, x)
        return remote(n1.at[0], n1.at[i], n1_s.at[i], n1_r.at[i], dev)

    n1_list = [(o, e) for o in [*far, 0] for e in range(2) if (o, e) != (0, 0)]
    for o, e in n1_list:
        n1c(o, e).start()
    for o, e in n1_list:
        n1c(o, e).wait_recv()
    part_sum = n1[0]
    for i in range(1, 2 * nz):
        part_sum = part_sum + n1[i]
    n2[0] = part_sum

    def n2c(o):
        return remote(n2.at[0], n2.at[o], n2_s.at[o], n2_r.at[o], at(yo(o), z, c, x))

    for o in range(1, ny):
        n2c(o).start()
    swap.wait_recv()
    for o in range(1, ny):
        n2c(o).wait_recv()
    part_sum = n2[0]
    for o in range(1, ny):
        part_sum = part_sum + n2[o]
    square_sum = jnp.sum(jnp.sum(part_sum, axis=1, keepdims=True), axis=0, keepdims=True)
    clip = jnp.minimum(1.0, max_norm / (jnp.sqrt(square_sum) + norm_eps))

    theirs = swr[0:6, :]
    gl = clip * jnp.where(c == 0, mine, theirs)
    gr = clip * jnp.where(c == 0, theirs, mine)
    nm, nf, ns = adam(gl, mrec[:, 0:512], frec[:, 0:512], srec[:, 0:512], weight_decay_rate)
    omrec[:, 0:512] = nm
    ofrec[:, 0:512] = nf
    osrec[:, 0:512] = ns
    hb[0, 0:6, :] = nm
    nm, nf, ns = adam(
        gr[:, 0:256], mrec[:, 512:768], frec[:, 512:768], srec[:, 512:768], weight_decay_rate
    )
    omrec[:, 512:768] = nm
    ofrec[:, 512:768] = nf
    osrec[:, 512:768] = ns
    hb[1, 0:6, 0:256] = nm
    nm, nf, ns = adam(gr[:, 256:512], mfac[...], ffac[...], sfac[...], weight_decay_rate)
    omfac[...] = nm
    offac[...] = nf
    osfac[...] = ns
    hb[1, 0:6, 256:512] = nm
    nm, nf, ns = adam(clip * my_ch, chs[0:1, :], chs[1:2, :], chs[2:3, :], 0.0)
    och[0:1, :] = nm
    och[1:2, :] = nf
    och[2:3, :] = ns
    for h in range(2):
        hb[h, 6:8, :] = jnp.zeros((2, 512), f32)
        hb[h, 6:7, 0:128] = nm

    aswap = remote(hb.at[d], ar, ag_sem.at[0], ag_sem.at[1], partner)
    aswap.start()
    bb[8:16, :] = jnp.zeros((8, 512), f32)
    asm[cr : cr + 16, :] = jnp.zeros((16, 512), f32)
    aswap.wait_recv()
    kept = hb[c]
    got = ar[...]
    r0 = jnp.where(c == 0, kept, got)
    r1 = jnp.where(c == 0, got, kept)
    bb[0:6, :] = r0[0:6, :]
    bb[6:12, :] = r1[0:6, :]
    bb[12:13, 0:128] = r0[6:7, 0:128]
    bb[12:13, 128:256] = r1[6:7, 0:128]
    zag[z] = bb[...].astype(bf16)

    def zg(o):
        return remote(zag.at[z], zag.at[z], zag_s.at[o - 1], zag_r.at[o - 1], at(y, zo(o), c, x))

    for o in far:
        zg(o).start()
    for i, ref in enumerate((omch, ofch, osch)):
        for r in range(6):
            ref[r : r + 1, :] = och[i : i + 1, 16 * r : 16 * r + 16]
    for o in reversed(far):
        zg(o).wait_recv()
    for zz in range(nz):
        blk = zag[zz].astype(f32)
        asm[12 * zz : 12 * zz + 12, :] = blk[0:12, :]
        asm[cr + zz : cr + zz + 1, 0:256] = blk[12:13, 0:256]
    w[c, y, 0] = asm[:, 0:256].astype(bf16)
    w[c, y, 1] = asm[:, 256:512].astype(bf16)

    def grow(h):
        return cr + 16 if h == 0 else cr

    def yg(st, s):
        dirn, h = STREAMS[st]
        blk = w.at[c, yo(-dirn * s), h, pl.ds(0, grow(h)), :]
        return remote(blk, blk, yag_s.at[st, s], yag_r.at[st, s], at(yo(dirn), z, c, x))

    def to_partner(k, h, ss, rr):
        blk = w.at[c, k, h, pl.ds(0, cr), :]
        return remote(blk, blk, ss, rr, partner)

    def pc(st, s):
        dirn, h = STREAMS[st]
        return to_partner(yo(-dirn * (s + 1)), h, pc_s.at[st, s], pc_r.at[st, s])

    def po(h):
        return to_partner(y, h, po_s.at[h], po_r.at[h])

    steps = [half if v else half - 1 for v in LONG]
    for st in (0, 2, 1, 3):
        yg(st, 0).start()
    po(0).start()
    po(1).start()
    for s in range(half):
        for st in (0, 2, 1, 3):
            if s < steps[st]:
                yg(st, s).wait_recv()
                if s + 1 < steps[st]:
                    yg(st, s + 1).start()
                pc(st, s).start()
    for h in range(2):
        po(h).wait_recv()
    for st in range(4):
        for s in range(steps[st]):
            pc(st, s).wait_recv()
    for k in range(ny):
        r = slice(cr * k, cr * k + cr)
        wrec[r, 0:256] = w[0, k, 0, 0:cr, :]
        wrec[r, 256:512] = w[0, k, 1, 0:cr, :]
        wrec[r, 512:768] = w[1, k, 0, 0:cr, :]
        wfac[r, :] = w[1, k, 1, 0:cr, :]
        wch[nz * k : nz * k + nz, :] = w[c, k, 0, cr : cr + 16, :].astype(f32)[0:nz, :]

    for i in range(ny):
        pair0(i).wait_send()
        pair1(i, True).wait_send()
    chc.wait_send()
    for st in range(4):
        for s in range(0 if LONG[st] else 1, half):
            rs(st, s).wait_send()
        for s in range(steps[st]):
            yg(st, s).wait_send()
            pc(st, s).wait_send()
    for o in range(1, nz):
        zc(o).wait_send()
        zg(o).wait_send()
    for o in range(1, nx):
        xc(o).wait_send()
    for o, e in n1_list:
        n1c(o, e).wait_send()
    for o in range(1, ny):
        n2c(o).wait_send()
    swap.wait_send()
    aswap.wait_send()
    for h in range(2):
        po(h).wait_send()


def write_out(*refs):
    n = (len(refs) - 1) // 2
    sem = refs[-1]
    copies = [
        pltpu.make_async_copy(refs[i], refs[n + i], sem.at[i]) for i in range(n)
    ]
    for copy in copies:
        copy.start()
    for copy in copies:
        copy.wait()


def body(ny, nz, nx, rec, fac, chan, mrec, mfac, mch, frec, ffac, fch, srec, sfac, sch):
    cr = 12 * nz
    rows = cr * ny
    sd = jax.ShapeDtypeStruct
    chg = jnp.sum(chan, axis=(0, 1, 2), dtype=f32).reshape(ny * nz, 2, 96)
    chg = jnp.pad(chg, ((0, 0), (0, 0), (0, 32))).reshape(ny * nz, 256)
    vm = pl.BlockSpec(memory_space=pltpu.VMEM)
    hbm = pl.BlockSpec(memory_space=pltpu.HBM)
    dma = pltpu.SemaphoreType.DMA
    half = ny // 2
    V = pltpu.VMEM
    out = pl.pallas_call(
        functools.partial(kernel, ny, nz, nx),
        out_shape=(
            sd((rows, 768), bf16), sd((rows, 256), bf16), sd((ny * nz, 256), f32),
        )
        + (sd((6, 768), f32), sd((6, 256), f32), sd((6, 16), f32)) * 3,
        in_specs=[hbm, hbm] + [vm] * 10,
        out_specs=(vm,) * 12,
        scratch_shapes=[
            V((8, 128), f32), V((8, 128), f32),
            V((2, 2, rows, 256), bf16), V((2, 2, rows, 256), bf16), V((ny * nz, 256), f32),
            V((ny, 2, cr + nz, 256), f32), V((4, half, cr + nz, 256), f32),
            V((nz, 16, 512), f32), V((nz - 1, 16, 512), f32), V((nx, 16, 512), f32),
            V((16, 512), f32), V((8, 512), f32), V((8, 512), f32),
            V((2 * nz, 8, 128), f32), V((ny, 8, 128), f32), V((2, 8, 512), f32), V((8, 512), f32),
            V((16, 512), f32), V((nz, 16, 512), bf16), V((cr + 16, 512), f32),
            V((2, ny, 2, cr + 16, 256), bf16),
            dma((2,)), dma((2, ny)), dma((2, ny)), dma, dma,
            dma((4, half)), dma((4, half)), dma((nz - 1,)), dma((nz - 1,)),
            dma((nx - 1,)), dma((nx - 1,)), dma((2,)),
            dma((2 * nz,)), dma((2 * nz,)), dma((ny,)), dma((ny,)), dma((2,)),
            dma((nz - 1,)), dma((nz - 1,)), dma((4, half)), dma((4, half)),
            dma((4, half)), dma((4, half)), dma((2,)), dma((2,)),
        ],
        compiler_params=pltpu.CompilerParams(
            collective_id=0, has_side_effects=True, vmem_limit_bytes=48_000_000
        ),
    )(rec, fac, chg, mrec, mfac, mch, frec, ffac, fch, srec, sfac, sch)
    wch = out[2].reshape(ny * nz, 2, 128)[:, :, :96].reshape(rows, 16).astype(bf16)
    held = out[:2] + out[3:]
    final = pl.pallas_call(
        write_out,
        out_shape=tuple(sd(o.shape, o.dtype) for o in held),
        in_specs=[pl.BlockSpec(memory_space=pl.ANY)] * len(held),
        out_specs=(pl.BlockSpec(memory_space=pl.ANY),) * len(held),
        scratch_shapes=[dma((len(held),))],
        compiler_params=pltpu.CompilerParams(vmem_limit_bytes=1 << 20),
    )(*held)
    return (final[0], final[1], wch, *final[2:])


def solution(mesh, nz=NZ):
    nx = mesh.shape["rep"]
    ny = mesh.shape["dp"] // (2 * nz)
    grad = P("dp", "rep", None, None, None)
    row = P("dp", None)
    return jax.shard_map(
        functools.partial(body, ny, nz, nx),
        mesh=mesh,
        in_specs=(grad,) * 3 + (row,) * 9,
        out_specs=(P(),) * 3 + (row,) * 9,
        check_vma=False,
    )
```

```python
import functools

import jax
import jax.numpy as jnp
from jax import lax
from jax.experimental import pallas as pl
from jax.experimental.pallas import tpu as pltpu
from jax.sharding import PartitionSpec as P

STEP = 20
NZ = 8

beta_one = 0.9
beta_two = 0.99
adam_eps = 1e-08
learn_rate = 0.001
weight_decay_rate = 0.1
max_norm = 1.0
norm_eps = 1e-06

MESH = pl.DeviceIdType.MESH
f32 = jnp.float32
bf16 = jnp.bfloat16

STREAMS = ((1, 0), (1, 1), (-1, 1), (-1, 0))
LONG = (True, False, True, False)


def adam(g, master, first, second, decay):
    new_first = beta_one * first + (1.0 - beta_one) * g
    new_second = beta_two * second + (1.0 - beta_two) * g * g
    update = (
        new_first
        / (1.0 - beta_one**STEP)
        / (jnp.sqrt(new_second / (1.0 - beta_two**STEP)) + adam_eps)
    )
    new_master = master - learn_rate * (update + decay * master)
    return new_master, new_first, new_second


def kernel(
    ny, nz, nx,
    rec, fac, chg, mrec, mfac, mch, frec, ffac, fch, srec, sfac, sch,
    wrec, wfac, wch, omrec, omfac, omch, ofrec, offac, ofch, osrec, osfac, osch,
    chs, och, own, part, chp, tmp, acc, acz, rbuf, rbuz, zs, zr, ys, yr, xb, sb, sws, swr, n1, n2, hb, ar, bb, zag, asm, w,
    own_sem, pair_s, pair_r, chp_s, chp_r, rs_s, rs_r, rz_s, rz_r, z_s, z_r, y_s, y_r, x_s, x_r, sw_sem,
    n1_s, n1_r, n2_s, n2_r, ag_sem, zag_s, zag_r, yag_s, yag_r, pc_s, pc_r, po_s, po_r,
):
    cr = 12 * nz
    half = ny // 2
    dp = lax.axis_index("dp")
    x = lax.axis_index("rep")
    c = lax.rem(dp, 2)
    z = lax.rem(dp // 2, nz)
    y = dp // (2 * nz)
    d = 1 - c

    def at(yy, zz, cc, xx):
        return ((yy * nz + zz) * 2 + cc, xx)

    def yo(o):
        return lax.rem(y + o + ny, ny)

    def zo(o):
        return lax.rem(z + o, nz)

    def xo(o):
        return lax.rem(x + o, nx)

    def remote(src, dst, ss, rs, dev):
        return pltpu.make_async_remote_copy(
            src_ref=src, dst_ref=dst, send_sem=ss, recv_sem=rs, device_id=dev, device_id_type=MESH
        )

    partner = at(y, z, d, x)

    own0 = pltpu.make_async_copy(
        rec.at[0, 0, :, :, pl.ds(pl.multiple_of(c * 512, 256), 256)], own.at[0], own_sem.at[0]
    )
    own0.start()

    @pl.when(c == 0)
    def _():
        pltpu.make_async_copy(rec.at[0, 0, :, :, pl.ds(256, 256)], own.at[1], own_sem.at[1]).start()

    @pl.when(c == 1)
    def _():
        pltpu.make_async_copy(fac.at[0, 0], own.at[1], own_sem.at[1]).start()

    barrier = pltpu.get_barrier_semaphore()
    peers = [partner]
    for o in range(1, nz):
        peers += [at(y, zo(o), c, x), at(y, zo(o), d, x)]
    for o in range(1, ny):
        peers.append(at(yo(o), z, c, x))
    for o in range(1, nx):
        peers.append(at(y, z, c, xo(o)))
    for dev in peers:
        pl.semaphore_signal(barrier, inc=1, device_id=dev, device_id_type=MESH)
    chs[...] = jnp.zeros_like(chs)
    for i, ref in enumerate((mch, fch, sch)):
        for r in range(6):
            chs[i : i + 1, 16 * r : 16 * r + 16] = ref[r : r + 1, :]
    pl.semaphore_wait(barrier, len(peers))

    order = [half]
    for o in range(half - 1, 0, -1):
        order += [o, ny - o]
    order.append(0)

    def rows_of(k):
        return pl.ds(pl.multiple_of(k * cr, 16), cr)

    def pair0(i):
        k = yo(order[i])
        return remote(
            rec.at[0, 0, :, rows_of(k), pl.ds(pl.multiple_of(d * 512, 256), 256)],
            part.at[0, :, rows_of(k), :], pair_s.at[0, i], pair_r.at[0, i], partner,
        )

    def pair1(i, to_fac):
        k = yo(order[i])
        if to_fac:
            src = fac.at[0, 0, :, rows_of(k), :]
        else:
            src = rec.at[0, 0, :, rows_of(k), pl.ds(256, 256)]
        return remote(src, part.at[1, :, rows_of(k), :], pair_s.at[1, i], pair_r.at[1, i], partner)

    chc = remote(chg, chp, chp_s, chp_r, partner)
    for i in range(ny):
        pair0(i).start()

        @pl.when(d == 1)
        def _():
            pair1(i, True).start()

        @pl.when(d == 0)
        def _():
            pair1(i, False).start()

        if i == 0:
            chc.start()

    own0.wait()
    pltpu.make_async_copy(fac.at[0, 0], own.at[1], own_sem.at[1]).wait()
    chc.wait_recv()

    def pair_sum(h, r):
        return (own[h, 0, r, :].astype(f32) + own[h, 1, r, :].astype(f32)) + (
            part[h, 0, r, :].astype(f32) + part[h, 1, r, :].astype(f32)
        )

    def chip_sum(i):
        k = yo(order[i])
        pair0(i).wait_recv()
        s = pair_sum(0, rows_of(k))
        r8 = pl.ds(pl.multiple_of(k * nz, nz), nz)
        ch = chg[r8, :] + chp[r8, :]
        for u in range(2):
            acc[k, u, 0:cr, :] = s[:, 128 * u : 128 * u + 128]
            acc[k, u, cr : cr + nz, :] = ch[:, 128 * u : 128 * u + 128]

    def chip_sum_z():
        for i in range(ny):
            pair1(i, True).wait_recv()
        for k in range(ny):
            tmp[k] = pair_sum(1, slice(cr * k, cr * k + cr))
            for zz in range(nz):
                for u in range(2):
                    acz[zz, u, 12 * k : 12 * k + 12, :] = tmp[
                        k, 12 * zz : 12 * zz + 12, 128 * u : 128 * u + 128
                    ]

    def rs(st, s):
        dirn, u = STREAMS[st]
        return remote(
            acc.at[yo(dirn * (half - s)), u], rbuf.at[st, s],
            rs_s.at[st, s], rs_r.at[st, s], at(yo(dirn), z, c, x),
        )

    def rz(st, s):
        dirn, u = STREAMS[st]
        return remote(
            acz.at[zo(dirn * (half - s) + nz), u], rbuz.at[st, s],
            rz_s.at[st, s], rz_r.at[st, s], at(y, zo(dirn + nz), c, x),
        )

    chip_sum(0)
    rs(0, 0).start()
    rs(2, 0).start()
    done = 1
    if half > 1:
        chip_sum(1)
        rs(1, 1).start()
        chip_sum(2)
        rs(3, 1).start()
        done = 3
    chip_sum_z()
    rz(0, 0).start()
    rz(2, 0).start()
    if half > 1:
        rz(1, 1).start()
        rz(3, 1).start()
    for s in range(1, half):
        for st in (0, 2, 1, 3):
            if s == 1 and not LONG[st]:
                continue
            dirn, u = STREAMS[st]
            rs(st, s - 1).wait_recv()
            k = yo(dirn * (half - s))
            acc[k, u] += rbuf[st, s - 1]
            rs(st, s).start()
        while done < min(2 * s + 3, ny):
            chip_sum(done)
            done += 1
        for st in (0, 2, 1, 3):
            if s == 1 and not LONG[st]:
                continue
            dirn, u = STREAMS[st]
            rz(st, s - 1).wait_recv()
            k = zo(dirn * (half - s) + nz)
            acz[k, u] += rbuz[st, s - 1]
            rz(st, s).start()
    while done < ny:
        chip_sum(done)
        done += 1
    zs[:, 8:16, :] = jnp.zeros((nz, 8, 256), f32)
    ys[:, 8:16, :] = jnp.zeros((ny, 8, 256), f32)

    far = sorted(range(1, nz), key=lambda o: -min(o, nz - o))

    def zc(o):
        return remote(zs.at[zo(o)], zr.at[o - 1], z_s.at[o - 1], z_r.at[o - 1], at(y, zo(o), c, x))

    def yc(o):
        return remote(ys.at[yo(o)], yr.at[o - 1], y_s.at[o - 1], y_r.at[o - 1], at(yo(o), z, c, x))

    for u, sts in ((0, (0, 3)), (1, (2, 1))):
        for st in sts:
            rs(st, half - 1).wait_recv()
        acc[y, u] = acc[y, u] + (rbuf[sts[0], half - 1] + rbuf[sts[1], half - 1])
        for zz in range(nz):
            lanes = slice(128 * u, 128 * u + 128)
            zs[zz, 0:12, lanes] = acc[y, u, 12 * zz : 12 * zz + 12, :]
            zs[zz, 12:13, lanes] = acc[y, u, cr + zz : cr + zz + 1, :]
    for o in far:
        zc(o).start()
    for u, sts in ((0, (0, 3)), (1, (2, 1))):
        for st in sts:
            rz(st, half - 1).wait_recv()
        acz[z, u] = acz[z, u] + (rbuz[sts[0], half - 1] + rbuz[sts[1], half - 1])
        for yy in range(ny):
            ys[yy, 0:12, 128 * u : 128 * u + 128] = acz[z, u, 12 * yy : 12 * yy + 12, :]
    for o in far:
        yc(o).start()
    total = zs[z]
    for o in reversed(far):
        zc(o).wait_recv()
        total = total + zr[o - 1]
    xb[x, :, 0:256] = total
    total = ys[y]
    for o in reversed(far):
        yc(o).wait_recv()
        total = total + yr[o - 1]
    xb[x, :, 256:512] = total

    def xc(o):
        return remote(xb.at[x], xb.at[x], x_s.at[o - 1], x_r.at[o - 1], at(y, z, c, xo(o)))

    for o in range(1, nx):
        xc(o).start()
    for o in range(1, nx):
        xc(o).wait_recv()
    total = xb[0]
    for o in range(1, nx):
        total = total + xb[o]
    sb[...] = total

    low = sb[0:6, :]
    high = sb[6:12, :]
    mine = jnp.where(c == 0, low, high)
    sws[0:6, :] = jnp.where(c == 0, high, low)
    sws[6:8, :] = jnp.zeros((2, 512), f32)
    swap = remote(sws, swr, sw_sem.at[0], sw_sem.at[1], partner)
    swap.start()

    my_ch = jnp.where(c == 0, sb[12:13, 0:128], sb[12:13, 128:256])
    sq = sb[0:8, :] * sb[0:8, :]
    sq = sq[:, 0:128] + sq[:, 128:256] + (sq[:, 256:384] + sq[:, 384:512])
    sh = sb[8:16, :] * sb[8:16, :]
    sh = sh[:, 0:128] + sh[:, 128:256] + (sh[:, 256:384] + sh[:, 384:512])
    row = lax.broadcasted_iota(jnp.int32, (8, 128), 0)
    sh = jnp.where(row < 4, sh, 0.0)
    ch_sq = jnp.where(row == 0, jnp.broadcast_to(my_ch * my_ch, (8, 128)), 0.0)
    n1[0] = sq + sh + ch_sq

    def n1c(o, e):
        i = 2 * o + e
        dev = at(y, zo(o), c if e == 0 else d, x)
        return remote(n1.at[0], n1.at[i], n1_s.at[i], n1_r.at[i], dev)

    n1_list = [(o, e) for o in [*far, 0] for e in range(2) if (o, e) != (0, 0)]
    for o, e in n1_list:
        n1c(o, e).start()
    for o, e in n1_list:
        n1c(o, e).wait_recv()
    part_sum = n1[0]
    for i in range(1, 2 * nz):
        part_sum = part_sum + n1[i]
    n2[0] = part_sum

    def n2c(o):
        return remote(n2.at[0], n2.at[o], n2_s.at[o], n2_r.at[o], at(yo(o), z, c, x))

    for o in range(1, ny):
        n2c(o).start()
    swap.wait_recv()
    for o in range(1, ny):
        n2c(o).wait_recv()
    part_sum = n2[0]
    for o in range(1, ny):
        part_sum = part_sum + n2[o]
    square_sum = jnp.sum(jnp.sum(part_sum, axis=1, keepdims=True), axis=0, keepdims=True)
    clip = jnp.minimum(1.0, max_norm / (jnp.sqrt(square_sum) + norm_eps))

    theirs = swr[0:6, :]
    gl = clip * jnp.where(c == 0, mine, theirs)
    gr = clip * jnp.where(c == 0, theirs, mine)
    nm, nf, ns = adam(gl, mrec[:, 0:512], frec[:, 0:512], srec[:, 0:512], weight_decay_rate)
    omrec[:, 0:512] = nm
    ofrec[:, 0:512] = nf
    osrec[:, 0:512] = ns
    hb[0, 0:6, :] = nm
    nm, nf, ns = adam(
        gr[:, 0:256], mrec[:, 512:768], frec[:, 512:768], srec[:, 512:768], weight_decay_rate
    )
    omrec[:, 512:768] = nm
    ofrec[:, 512:768] = nf
    osrec[:, 512:768] = ns
    hb[1, 0:6, 0:256] = nm
    nm, nf, ns = adam(gr[:, 256:512], mfac[...], ffac[...], sfac[...], weight_decay_rate)
    omfac[...] = nm
    offac[...] = nf
    osfac[...] = ns
    hb[1, 0:6, 256:512] = nm
    nm, nf, ns = adam(clip * my_ch, chs[0:1, :], chs[1:2, :], chs[2:3, :], 0.0)
    och[0:1, :] = nm
    och[1:2, :] = nf
    och[2:3, :] = ns
    for h in range(2):
        hb[h, 6:8, :] = jnp.zeros((2, 512), f32)
        hb[h, 6:7, 0:128] = nm

    aswap = remote(hb.at[d], ar, ag_sem.at[0], ag_sem.at[1], partner)
    aswap.start()
    bb[8:16, :] = jnp.zeros((8, 512), f32)
    asm[cr : cr + 16, :] = jnp.zeros((16, 512), f32)
    aswap.wait_recv()
    kept = hb[c]
    got = ar[...]
    r0 = jnp.where(c == 0, kept, got)
    r1 = jnp.where(c == 0, got, kept)
    bb[0:6, :] = r0[0:6, :]
    bb[6:12, :] = r1[0:6, :]
    bb[12:13, 0:128] = r0[6:7, 0:128]
    bb[12:13, 128:256] = r1[6:7, 0:128]
    zag[z] = bb[...].astype(bf16)

    def zg(o):
        return remote(zag.at[z], zag.at[z], zag_s.at[o - 1], zag_r.at[o - 1], at(y, zo(o), c, x))

    for o in far:
        zg(o).start()
    for i, ref in enumerate((omch, ofch, osch)):
        for r in range(6):
            ref[r : r + 1, :] = och[i : i + 1, 16 * r : 16 * r + 16]
    for o in reversed(far):
        zg(o).wait_recv()
    for zz in range(nz):
        blk = zag[zz].astype(f32)
        asm[12 * zz : 12 * zz + 12, :] = blk[0:12, :]
        asm[cr + zz : cr + zz + 1, 0:256] = blk[12:13, 0:256]
    w[c, y, 0] = asm[:, 0:256].astype(bf16)
    w[c, y, 1] = asm[:, 256:512].astype(bf16)

    def grow(h):
        return cr + 16 if h == 0 else cr

    def yg(st, s):
        dirn, h = STREAMS[st]
        blk = w.at[c, yo(-dirn * s), h, pl.ds(0, grow(h)), :]
        return remote(blk, blk, yag_s.at[st, s], yag_r.at[st, s], at(yo(dirn), z, c, x))

    def to_partner(k, h, ss, rr):
        blk = w.at[c, k, h, pl.ds(0, cr), :]
        return remote(blk, blk, ss, rr, partner)

    def pc(st, s):
        dirn, h = STREAMS[st]
        return to_partner(yo(-dirn * (s + 1)), h, pc_s.at[st, s], pc_r.at[st, s])

    def po(h):
        return to_partner(y, h, po_s.at[h], po_r.at[h])

    steps = [half if v else half - 1 for v in LONG]
    for st in (0, 2, 1, 3):
        yg(st, 0).start()
    po(0).start()
    po(1).start()
    for s in range(half):
        for st in (0, 2, 1, 3):
            if s < steps[st]:
                yg(st, s).wait_recv()
                if s + 1 < steps[st]:
                    yg(st, s + 1).start()
                pc(st, s).start()
    for h in range(2):
        po(h).wait_recv()
    for st in range(4):
        for s in range(steps[st]):
            pc(st, s).wait_recv()
    for k in range(ny):
        r = slice(cr * k, cr * k + cr)
        wrec[r, 0:256] = w[0, k, 0, 0:cr, :]
        wrec[r, 256:512] = w[0, k, 1, 0:cr, :]
        wrec[r, 512:768] = w[1, k, 0, 0:cr, :]
        wfac[r, :] = w[1, k, 1, 0:cr, :]
        wch[nz * k : nz * k + nz, :] = w[c, k, 0, cr : cr + 16, :].astype(f32)[0:nz, :]

    for i in range(ny):
        pair0(i).wait_send()
        pair1(i, True).wait_send()
    chc.wait_send()
    for st in range(4):
        for s in range(0 if LONG[st] else 1, half):
            rs(st, s).wait_send()
            rz(st, s).wait_send()
        for s in range(steps[st]):
            yg(st, s).wait_send()
            pc(st, s).wait_send()
    for o in range(1, nz):
        zc(o).wait_send()
        yc(o).wait_send()
        zg(o).wait_send()
    for o in range(1, nx):
        xc(o).wait_send()
    for o, e in n1_list:
        n1c(o, e).wait_send()
    for o in range(1, ny):
        n2c(o).wait_send()
    swap.wait_send()
    aswap.wait_send()
    for h in range(2):
        po(h).wait_send()


def write_out(*refs):
    n = (len(refs) - 1) // 2
    sem = refs[-1]
    copies = [
        pltpu.make_async_copy(refs[i], refs[n + i], sem.at[i]) for i in range(n)
    ]
    for copy in copies:
        copy.start()
    for copy in copies:
        copy.wait()


def body(ny, nz, nx, rec, fac, chan, mrec, mfac, mch, frec, ffac, fch, srec, sfac, sch):
    cr = 12 * nz
    rows = cr * ny
    sd = jax.ShapeDtypeStruct
    chg = jnp.sum(chan, axis=(0, 1, 2), dtype=f32).reshape(ny * nz, 2, 96)
    chg = jnp.pad(chg, ((0, 0), (0, 0), (0, 32))).reshape(ny * nz, 256)
    vm = pl.BlockSpec(memory_space=pltpu.VMEM)
    hbm = pl.BlockSpec(memory_space=pltpu.HBM)
    dma = pltpu.SemaphoreType.DMA
    half = ny // 2
    V = pltpu.VMEM
    out = pl.pallas_call(
        functools.partial(kernel, ny, nz, nx),
        out_shape=(
            sd((rows, 768), bf16), sd((rows, 256), bf16), sd((ny * nz, 256), f32),
        )
        + (sd((6, 768), f32), sd((6, 256), f32), sd((6, 16), f32)) * 3,
        in_specs=[hbm, hbm] + [vm] * 10,
        out_specs=(vm,) * 12,
        scratch_shapes=[
            V((8, 128), f32), V((8, 128), f32),
            V((2, 2, rows, 256), bf16), V((2, 2, rows, 256), bf16), V((ny * nz, 256), f32),
            V((ny, cr, 256), f32),
            V((ny, 2, cr + nz, 128), f32), V((nz, 2, cr, 128), f32),
            V((4, half, cr + nz, 128), f32), V((4, half, cr, 128), f32),
            V((nz, 16, 256), f32), V((nz - 1, 16, 256), f32),
            V((ny, 16, 256), f32), V((ny - 1, 16, 256), f32), V((nx, 16, 512), f32),
            V((16, 512), f32), V((8, 512), f32), V((8, 512), f32),
            V((2 * nz, 8, 128), f32), V((ny, 8, 128), f32), V((2, 8, 512), f32), V((8, 512), f32),
            V((16, 512), f32), V((nz, 16, 512), bf16), V((cr + 16, 512), f32),
            V((2, ny, 2, cr + 16, 256), bf16),
            dma((2,)), dma((2, ny)), dma((2, ny)), dma, dma,
            dma((4, half)), dma((4, half)), dma((4, half)), dma((4, half)),
            dma((nz - 1,)), dma((nz - 1,)), dma((ny - 1,)), dma((ny - 1,)),
            dma((nx - 1,)), dma((nx - 1,)), dma((2,)),
            dma((2 * nz,)), dma((2 * nz,)), dma((ny,)), dma((ny,)), dma((2,)),
            dma((nz - 1,)), dma((nz - 1,)), dma((4, half)), dma((4, half)),
            dma((4, half)), dma((4, half)), dma((2,)), dma((2,)),
        ],
        compiler_params=pltpu.CompilerParams(
            collective_id=0, has_side_effects=True, vmem_limit_bytes=48_000_000
        ),
    )(rec, fac, chg, mrec, mfac, mch, frec, ffac, fch, srec, sfac, sch)
    wch = out[2].reshape(ny * nz, 2, 128)[:, :, :96].reshape(rows, 16).astype(bf16)
    held = out[:2] + out[3:]
    final = pl.pallas_call(
        write_out,
        out_shape=tuple(sd(o.shape, o.dtype) for o in held),
        in_specs=[pl.BlockSpec(memory_space=pl.ANY)] * len(held),
        out_specs=(pl.BlockSpec(memory_space=pl.ANY),) * len(held),
        scratch_shapes=[dma((len(held),))],
        compiler_params=pltpu.CompilerParams(vmem_limit_bytes=1 << 20),
    )(*held)
    return (final[0], final[1], wch, *final[2:])


def solution(mesh, nz=NZ):
    nx = mesh.shape["rep"]
    ny = mesh.shape["dp"] // (2 * nz)
    assert ny == nz and ny % 2 == 0
    grad = P("dp", "rep", None, None, None)
    row = P("dp", None)
    return jax.shard_map(
        functools.partial(body, ny, nz, nx),
        mesh=mesh,
        in_specs=(grad,) * 3 + (row,) * 9,
        out_specs=(P(),) * 3 + (row,) * 9,
        check_vma=False,
    )
```

```python
import functools

import jax
import jax.numpy as jnp
from jax import lax
from jax.experimental import pallas as pl
from jax.experimental.pallas import tpu as pltpu
from jax.sharding import PartitionSpec as P

STEP = 20
NZ = 8

beta_one = 0.9
beta_two = 0.99
adam_eps = 1e-08
learn_rate = 0.001
weight_decay_rate = 0.1
max_norm = 1.0
norm_eps = 1e-06

MESH = pl.DeviceIdType.MESH
f32 = jnp.float32
bf16 = jnp.bfloat16

STREAMS = ((1, 0), (1, 1), (-1, 1), (-1, 0))
LONG = (True, False, True, False)


def adam(g, master, first, second, decay):
    new_first = beta_one * first + (1.0 - beta_one) * g
    new_second = beta_two * second + (1.0 - beta_two) * g * g
    update = (
        new_first
        / (1.0 - beta_one**STEP)
        / (jnp.sqrt(new_second / (1.0 - beta_two**STEP)) + adam_eps)
    )
    new_master = master - learn_rate * (update + decay * master)
    return new_master, new_first, new_second


def kernel(
    ny, nz, nx,
    rec, fac, chg, mrec, mfac, mch, frec, ffac, fch, srec, sfac, sch,
    w, wch, omrec, omfac, omch, ofrec, offac, ofch, osrec, osfac, osch,
    chs, och, own, part, chp, tmp, acc, acz, rbuf, rbuz, zs, zr, ys, yr, xb, sb, sws, swr, n1, n2, hb, ar, bb, zag, asm,
    own_sem, pair_s, pair_r, chp_s, chp_r, rs_s, rs_r, rz_s, rz_r, z_s, z_r, y_s, y_r, x_s, x_r, sw_sem,
    n1_s, n1_r, n2_s, n2_r, ag_sem, zag_s, zag_r, yag_s, yag_r, pc_s, pc_r, po_s, po_r,
):
    cr = 12 * nz
    half = ny // 2
    dp = lax.axis_index("dp")
    x = lax.axis_index("rep")
    c = lax.rem(dp, 2)
    z = lax.rem(dp // 2, nz)
    y = dp // (2 * nz)
    d = 1 - c

    def at(yy, zz, cc, xx):
        return ((yy * nz + zz) * 2 + cc, xx)

    def yo(o):
        return lax.rem(y + o + ny, ny)

    def zo(o):
        return lax.rem(z + o, nz)

    def xo(o):
        return lax.rem(x + o, nx)

    def remote(src, dst, ss, rs, dev):
        return pltpu.make_async_remote_copy(
            src_ref=src, dst_ref=dst, send_sem=ss, recv_sem=rs, device_id=dev, device_id_type=MESH
        )

    partner = at(y, z, d, x)

    own0 = pltpu.make_async_copy(
        rec.at[0, 0, :, :, pl.ds(pl.multiple_of(c * 512, 256), 256)], own.at[0], own_sem.at[0]
    )
    own0.start()

    @pl.when(c == 0)
    def _():
        pltpu.make_async_copy(rec.at[0, 0, :, :, pl.ds(256, 256)], own.at[1], own_sem.at[1]).start()

    @pl.when(c == 1)
    def _():
        pltpu.make_async_copy(fac.at[0, 0], own.at[1], own_sem.at[1]).start()

    barrier = pltpu.get_barrier_semaphore()
    peers = [partner]
    for o in range(1, nz):
        peers += [at(y, zo(o), c, x), at(y, zo(o), d, x)]
    for o in range(1, ny):
        peers.append(at(yo(o), z, c, x))
    for o in range(1, nx):
        peers.append(at(y, z, c, xo(o)))
    for dev in peers:
        pl.semaphore_signal(barrier, inc=1, device_id=dev, device_id_type=MESH)
    chs[...] = jnp.zeros_like(chs)
    for i, ref in enumerate((mch, fch, sch)):
        for r in range(6):
            chs[i : i + 1, 16 * r : 16 * r + 16] = ref[r : r + 1, :]
    pl.semaphore_wait(barrier, len(peers))

    order = [half]
    for o in range(half - 1, 0, -1):
        order += [o, ny - o]
    order.append(0)

    def rows_of(k):
        return pl.ds(pl.multiple_of(k * cr, 16), cr)

    def pair0(i):
        k = yo(order[i])
        return remote(
            rec.at[0, 0, :, rows_of(k), pl.ds(pl.multiple_of(d * 512, 256), 256)],
            part.at[0, :, rows_of(k), :], pair_s.at[0, i], pair_r.at[0, i], partner,
        )

    def pair1(i, to_fac):
        k = yo(order[i])
        if to_fac:
            src = fac.at[0, 0, :, rows_of(k), :]
        else:
            src = rec.at[0, 0, :, rows_of(k), pl.ds(256, 256)]
        return remote(src, part.at[1, :, rows_of(k), :], pair_s.at[1, i], pair_r.at[1, i], partner)

    chc = remote(chg, chp, chp_s, chp_r, partner)
    for i in range(ny):
        pair0(i).start()

        @pl.when(d == 1)
        def _():
            pair1(i, True).start()

        @pl.when(d == 0)
        def _():
            pair1(i, False).start()

        if i == 0:
            chc.start()

    own0.wait()
    pltpu.make_async_copy(fac.at[0, 0], own.at[1], own_sem.at[1]).wait()
    chc.wait_recv()

    def pair_sum(h, r):
        return (own[h, 0, r, :].astype(f32) + own[h, 1, r, :].astype(f32)) + (
            part[h, 0, r, :].astype(f32) + part[h, 1, r, :].astype(f32)
        )

    def chip_sum(i):
        k = yo(order[i])
        pair0(i).wait_recv()
        s = pair_sum(0, rows_of(k))
        r8 = pl.ds(pl.multiple_of(k * nz, nz), nz)
        ch = chg[r8, :] + chp[r8, :]
        for u in range(2):
            acc[k, u, 0:cr, :] = s[:, 128 * u : 128 * u + 128]
            acc[k, u, cr : cr + nz, :] = ch[:, 128 * u : 128 * u + 128]

    def chip_sum_z():
        for i in range(ny):
            pair1(i, True).wait_recv()
        for k in range(ny):
            tmp[k] = pair_sum(1, slice(cr * k, cr * k + cr))
            for zz in range(nz):
                for u in range(2):
                    acz[zz, u, 12 * k : 12 * k + 12, :] = tmp[
                        k, 12 * zz : 12 * zz + 12, 128 * u : 128 * u + 128
                    ]

    def rs(st, s):
        dirn, u = STREAMS[st]
        return remote(
            acc.at[yo(dirn * (half - s)), u], rbuf.at[st, s],
            rs_s.at[st, s], rs_r.at[st, s], at(yo(dirn), z, c, x),
        )

    def rz(st, s):
        dirn, u = STREAMS[st]
        return remote(
            acz.at[zo(dirn * (half - s) + nz), u], rbuz.at[st, s],
            rz_s.at[st, s], rz_r.at[st, s], at(y, zo(dirn + nz), c, x),
        )

    chip_sum(0)
    rs(0, 0).start()
    rs(2, 0).start()
    done = 1
    if half > 1:
        chip_sum(1)
        rs(1, 1).start()
        chip_sum(2)
        rs(3, 1).start()
        done = 3
    chip_sum_z()
    rz(0, 0).start()
    rz(2, 0).start()
    if half > 1:
        rz(1, 1).start()
        rz(3, 1).start()
    for s in range(1, half):
        for st in (0, 2, 1, 3):
            if s == 1 and not LONG[st]:
                continue
            dirn, u = STREAMS[st]
            rs(st, s - 1).wait_recv()
            k = yo(dirn * (half - s))
            acc[k, u] += rbuf[st, s - 1]
            rs(st, s).start()
        while done < min(2 * s + 3, ny):
            chip_sum(done)
            done += 1
        for st in (0, 2, 1, 3):
            if s == 1 and not LONG[st]:
                continue
            dirn, u = STREAMS[st]
            rz(st, s - 1).wait_recv()
            k = zo(dirn * (half - s) + nz)
            acz[k, u] += rbuz[st, s - 1]
            rz(st, s).start()
    while done < ny:
        chip_sum(done)
        done += 1
    zs[:, 8:16, :] = jnp.zeros((nz, 8, 256), f32)
    ys[:, 8:16, :] = jnp.zeros((ny, 8, 256), f32)

    far = sorted(range(1, nz), key=lambda o: -min(o, nz - o))

    def zc(o):
        return remote(zs.at[zo(o)], zr.at[o - 1], z_s.at[o - 1], z_r.at[o - 1], at(y, zo(o), c, x))

    def yc(o):
        return remote(ys.at[yo(o)], yr.at[o - 1], y_s.at[o - 1], y_r.at[o - 1], at(yo(o), z, c, x))

    for u, sts in ((0, (0, 3)), (1, (2, 1))):
        for st in sts:
            rs(st, half - 1).wait_recv()
        acc[y, u] = acc[y, u] + (rbuf[sts[0], half - 1] + rbuf[sts[1], half - 1])
        for zz in range(nz):
            lanes = slice(128 * u, 128 * u + 128)
            zs[zz, 0:12, lanes] = acc[y, u, 12 * zz : 12 * zz + 12, :]
            zs[zz, 12:13, lanes] = acc[y, u, cr + zz : cr + zz + 1, :]
    for o in far:
        zc(o).start()
    for u, sts in ((0, (0, 3)), (1, (2, 1))):
        for st in sts:
            rz(st, half - 1).wait_recv()
        acz[z, u] = acz[z, u] + (rbuz[sts[0], half - 1] + rbuz[sts[1], half - 1])
        for yy in range(ny):
            ys[yy, 0:12, 128 * u : 128 * u + 128] = acz[z, u, 12 * yy : 12 * yy + 12, :]
    for o in far:
        yc(o).start()
    total = zs[z]
    for o in reversed(far):
        zc(o).wait_recv()
        total = total + zr[o - 1]
    xb[x, :, 0:256] = total
    total = ys[y]
    for o in reversed(far):
        yc(o).wait_recv()
        total = total + yr[o - 1]
    xb[x, :, 256:512] = total

    def xc(o):
        return remote(xb.at[x], xb.at[x], x_s.at[o - 1], x_r.at[o - 1], at(y, z, c, xo(o)))

    for o in range(1, nx):
        xc(o).start()
    for o in range(1, nx):
        xc(o).wait_recv()
    total = xb[0]
    for o in range(1, nx):
        total = total + xb[o]
    sb[...] = total

    low = sb[0:6, :]
    high = sb[6:12, :]
    mine = jnp.where(c == 0, low, high)
    sws[0:6, :] = jnp.where(c == 0, high, low)
    sws[6:8, :] = jnp.zeros((2, 512), f32)
    swap = remote(sws, swr, sw_sem.at[0], sw_sem.at[1], partner)
    swap.start()

    my_ch = jnp.where(c == 0, sb[12:13, 0:128], sb[12:13, 128:256])
    sq = sb[0:8, :] * sb[0:8, :]
    sq = sq[:, 0:128] + sq[:, 128:256] + (sq[:, 256:384] + sq[:, 384:512])
    sh = sb[8:16, :] * sb[8:16, :]
    sh = sh[:, 0:128] + sh[:, 128:256] + (sh[:, 256:384] + sh[:, 384:512])
    row = lax.broadcasted_iota(jnp.int32, (8, 128), 0)
    sh = jnp.where(row < 4, sh, 0.0)
    ch_sq = jnp.where(row == 0, jnp.broadcast_to(my_ch * my_ch, (8, 128)), 0.0)
    n1[0] = sq + sh + ch_sq

    def n1c(o, e):
        i = 2 * o + e
        dev = at(y, zo(o), c if e == 0 else d, x)
        return remote(n1.at[0], n1.at[i], n1_s.at[i], n1_r.at[i], dev)

    n1_list = [(o, e) for o in [*far, 0] for e in range(2) if (o, e) != (0, 0)]
    for o, e in n1_list:
        n1c(o, e).start()
    for o, e in n1_list:
        n1c(o, e).wait_recv()
    part_sum = n1[0]
    for i in range(1, 2 * nz):
        part_sum = part_sum + n1[i]
    n2[0] = part_sum

    def n2c(o):
        return remote(n2.at[0], n2.at[o], n2_s.at[o], n2_r.at[o], at(yo(o), z, c, x))

    for o in range(1, ny):
        n2c(o).start()
    swap.wait_recv()
    for o in range(1, ny):
        n2c(o).wait_recv()
    part_sum = n2[0]
    for o in range(1, ny):
        part_sum = part_sum + n2[o]
    square_sum = jnp.sum(jnp.sum(part_sum, axis=1, keepdims=True), axis=0, keepdims=True)
    clip = jnp.minimum(1.0, max_norm / (jnp.sqrt(square_sum) + norm_eps))

    theirs = swr[0:6, :]
    gl = clip * jnp.where(c == 0, mine, theirs)
    gr = clip * jnp.where(c == 0, theirs, mine)
    nm, nf, ns = adam(gl, mrec[:, 0:512], frec[:, 0:512], srec[:, 0:512], weight_decay_rate)
    omrec[:, 0:512] = nm
    ofrec[:, 0:512] = nf
    osrec[:, 0:512] = ns
    hb[0, 0:6, :] = nm
    nm, nf, ns = adam(
        gr[:, 0:256], mrec[:, 512:768], frec[:, 512:768], srec[:, 512:768], weight_decay_rate
    )
    omrec[:, 512:768] = nm
    ofrec[:, 512:768] = nf
    osrec[:, 512:768] = ns
    hb[1, 0:6, 0:256] = nm
    nm, nf, ns = adam(gr[:, 256:512], mfac[...], ffac[...], sfac[...], weight_decay_rate)
    omfac[...] = nm
    offac[...] = nf
    osfac[...] = ns
    hb[1, 0:6, 256:512] = nm
    nm, nf, ns = adam(clip * my_ch, chs[0:1, :], chs[1:2, :], chs[2:3, :], 0.0)
    och[0:1, :] = nm
    och[1:2, :] = nf
    och[2:3, :] = ns
    for h in range(2):
        hb[h, 6:8, :] = jnp.zeros((2, 512), f32)
        hb[h, 6:7, 0:128] = nm

    aswap = remote(hb.at[d], ar, ag_sem.at[0], ag_sem.at[1], partner)
    aswap.start()
    bb[8:16, :] = jnp.zeros((8, 512), f32)
    asm[cr : cr + 16, :] = jnp.zeros((16, 512), f32)
    aswap.wait_recv()
    kept = hb[c]
    got = ar[...]
    r0 = jnp.where(c == 0, kept, got)
    r1 = jnp.where(c == 0, got, kept)
    bb[0:6, :] = r0[0:6, :]
    bb[6:12, :] = r1[0:6, :]
    bb[12:13, 0:128] = r0[6:7, 0:128]
    bb[12:13, 128:256] = r1[6:7, 0:128]
    zag[z] = bb[...].astype(bf16)

    def zg(o):
        return remote(zag.at[z], zag.at[z], zag_s.at[o - 1], zag_r.at[o - 1], at(y, zo(o), c, x))

    for o in far:
        zg(o).start()
    for i, ref in enumerate((omch, ofch, osch)):
        for r in range(6):
            ref[r : r + 1, :] = och[i : i + 1, 16 * r : 16 * r + 16]
    for o in reversed(far):
        zg(o).wait_recv()
    for zz in range(nz):
        blk = zag[zz].astype(f32)
        asm[12 * zz : 12 * zz + 12, :] = blk[0:12, :]
        asm[cr + zz : cr + zz + 1, 0:256] = blk[12:13, 0:256]
    w[c, y, 0] = asm[:, 0:256].astype(bf16)
    w[c, y, 1] = asm[:, 256:512].astype(bf16)

    def grow(h):
        return cr + 16 if h == 0 else cr

    def yg(st, s):
        dirn, h = STREAMS[st]
        blk = w.at[c, yo(-dirn * s), h, pl.ds(0, grow(h)), :]
        return remote(blk, blk, yag_s.at[st, s], yag_r.at[st, s], at(yo(dirn), z, c, x))

    def to_partner(k, h, ss, rr):
        blk = w.at[c, k, h, pl.ds(0, cr), :]
        return remote(blk, blk, ss, rr, partner)

    def pc(st, s):
        dirn, h = STREAMS[st]
        return to_partner(yo(-dirn * (s + 1)), h, pc_s.at[st, s], pc_r.at[st, s])

    def po(h):
        return to_partner(y, h, po_s.at[h], po_r.at[h])

    steps = [half if v else half - 1 for v in LONG]
    for st in (0, 2, 1, 3):
        yg(st, 0).start()
    po(0).start()
    po(1).start()
    for s in range(half):
        for st in (0, 2, 1, 3):
            if s < steps[st]:
                yg(st, s).wait_recv()
                if s + 1 < steps[st]:
                    yg(st, s + 1).start()
                pc(st, s).start()
    for k in range(ny):
        wch[nz * k : nz * k + nz, :] = w[c, k, 0, cr : cr + 16, :].astype(f32)[0:nz, :]

    for h in range(2):
        po(h).wait_recv()
    for st in range(4):
        for s in range(steps[st]):
            pc(st, s).wait_recv()

    for i in range(ny):
        pair0(i).wait_send()
        pair1(i, True).wait_send()
    chc.wait_send()
    for st in range(4):
        for s in range(0 if LONG[st] else 1, half):
            rs(st, s).wait_send()
            rz(st, s).wait_send()
        for s in range(steps[st]):
            yg(st, s).wait_send()
            pc(st, s).wait_send()
    for o in range(1, nz):
        zc(o).wait_send()
        yc(o).wait_send()
        zg(o).wait_send()
    for o in range(1, nx):
        xc(o).wait_send()
    for o, e in n1_list:
        n1c(o, e).wait_send()
    for o in range(1, ny):
        n2c(o).wait_send()
    swap.wait_send()
    aswap.wait_send()
    for h in range(2):
        po(h).wait_send()


def write_out(ny, cr, w, *refs):
    n = (len(refs) - 3) // 2
    wrec, wfac, sem = refs[n], refs[n + 1], refs[-1]
    pairs = [(refs[i], refs[n + 2 + i]) for i in range(n)]
    for k in range(ny):
        r = pl.ds(cr * k, cr)
        cut = pl.ds(0, cr)
        pairs += [
            (w.at[0, k, 0, cut, :], wrec.at[r, pl.ds(0, 256)]),
            (w.at[0, k, 1, cut, :], wrec.at[r, pl.ds(256, 256)]),
            (w.at[1, k, 0, cut, :], wrec.at[r, pl.ds(512, 256)]),
            (w.at[1, k, 1, cut, :], wfac.at[r, :]),
        ]
    copies = [pltpu.make_async_copy(p, q, sem.at[i]) for i, (p, q) in enumerate(pairs)]
    for copy in copies:
        copy.start()
    for copy in copies:
        copy.wait()


def body(ny, nz, nx, rec, fac, chan, mrec, mfac, mch, frec, ffac, fch, srec, sfac, sch):
    cr = 12 * nz
    rows = cr * ny
    sd = jax.ShapeDtypeStruct
    chg = jnp.sum(chan, axis=(0, 1, 2), dtype=f32).reshape(ny * nz, 2, 96)
    chg = jnp.pad(chg, ((0, 0), (0, 0), (0, 32))).reshape(ny * nz, 256)
    vm = pl.BlockSpec(memory_space=pltpu.VMEM)
    hbm = pl.BlockSpec(memory_space=pltpu.HBM)
    dma = pltpu.SemaphoreType.DMA
    half = ny // 2
    V = pltpu.VMEM
    out = pl.pallas_call(
        functools.partial(kernel, ny, nz, nx),
        out_shape=(
            sd((2, ny, 2, cr + 16, 256), bf16), sd((ny * nz, 256), f32),
        )
        + (sd((6, 768), f32), sd((6, 256), f32), sd((6, 16), f32)) * 3,
        in_specs=[hbm, hbm] + [vm] * 10,
        out_specs=(vm,) * 11,
        scratch_shapes=[
            V((8, 128), f32), V((8, 128), f32),
            V((2, 2, rows, 256), bf16), V((2, 2, rows, 256), bf16), V((ny * nz, 256), f32),
            V((ny, cr, 256), f32),
            V((ny, 2, cr + nz, 128), f32), V((nz, 2, cr, 128), f32),
            V((4, half, cr + nz, 128), f32), V((4, half, cr, 128), f32),
            V((nz, 16, 256), f32), V((nz - 1, 16, 256), f32),
            V((ny, 16, 256), f32), V((ny - 1, 16, 256), f32), V((nx, 16, 512), f32),
            V((16, 512), f32), V((8, 512), f32), V((8, 512), f32),
            V((2 * nz, 8, 128), f32), V((ny, 8, 128), f32), V((2, 8, 512), f32), V((8, 512), f32),
            V((16, 512), f32), V((nz, 16, 512), bf16), V((cr + 16, 512), f32),
            dma((2,)), dma((2, ny)), dma((2, ny)), dma, dma,
            dma((4, half)), dma((4, half)), dma((4, half)), dma((4, half)),
            dma((nz - 1,)), dma((nz - 1,)), dma((ny - 1,)), dma((ny - 1,)),
            dma((nx - 1,)), dma((nx - 1,)), dma((2,)),
            dma((2 * nz,)), dma((2 * nz,)), dma((ny,)), dma((ny,)), dma((2,)),
            dma((nz - 1,)), dma((nz - 1,)), dma((4, half)), dma((4, half)),
            dma((4, half)), dma((4, half)), dma((2,)), dma((2,)),
        ],
        compiler_params=pltpu.CompilerParams(
            collective_id=0, has_side_effects=True, vmem_limit_bytes=48_000_000
        ),
    )(rec, fac, chg, mrec, mfac, mch, frec, ffac, fch, srec, sfac, sch)
    wch = out[1].reshape(ny * nz, 2, 128)[:, :, :96].reshape(rows, 16).astype(bf16)
    anywhere = pl.BlockSpec(memory_space=pl.ANY)
    held = out[2:]
    final = pl.pallas_call(
        functools.partial(write_out, ny, cr),
        out_shape=(sd((rows, 768), bf16), sd((rows, 256), bf16))
        + tuple(sd(o.shape, o.dtype) for o in held),
        in_specs=[anywhere] * (1 + len(held)),
        out_specs=(anywhere,) * (2 + len(held)),
        scratch_shapes=[dma((4 * ny + len(held),))],
        compiler_params=pltpu.CompilerParams(vmem_limit_bytes=1 << 20),
    )(out[0], *held)
    return (final[0], final[1], wch, *final[2:])


def solution(mesh, nz=NZ):
    nx = mesh.shape["rep"]
    ny = mesh.shape["dp"] // (2 * nz)
    assert ny == nz and ny % 2 == 0
    grad = P("dp", "rep", None, None, None)
    row = P("dp", None)
    return jax.shard_map(
        functools.partial(body, ny, nz, nx),
        mesh=mesh,
        in_specs=(grad,) * 3 + (row,) * 9,
        out_specs=(P(),) * 3 + (row,) * 9,
        check_vma=False,
    )
```
